32 devices in a mesh: groups: 2 (over x), section: 16 (over z, y, core).
Axes of the slice: x: 2, y: 2, z: 4, core: 2. Of those that a mesh axis runs over, the one named last changes fastest.
Arguments:
- micro: bfloat16 [32, 192, 1024], P(('groups', 'section')), parts along dimension 0, may hold values from -6 to 6
- segment: int32 [32, 192], P(('groups', 'section')), parts along dimension 0, may hold values from 0 to 3, as said below
- gain: bfloat16 [16, 1024], P('section'), may hold values from 0.099609375 to 1.8984375
- w_query: bfloat16 [16, 1024, 2048], P('section'), may hold values from -0.1875 to 0.1875
- w_key: bfloat16 [16, 1024, 1024], P('section'), may hold values from -0.1875 to 0.1875
- w_value: bfloat16 [16, 1024, 1024], P('section'), may hold values from -0.1875 to 0.1875
- w_out: bfloat16 [16, 2048, 1024], P('section'), may hold values from -0.125 to 0.125
Outputs:
- result: bfloat16 [32, 192, 1024], P(('groups', 'section')), parts along dimension 0
The draws below stay inside these ranges and needn't reach their ends.
There are 2 independent parts, one for each index of `groups`. The reference program is written for one: setup_inputs(seed, part) draws one part's arguments, and reference() takes and returns one part's arrays. A program takes and returns all parts, laid end to end along the dimension named above; an argument that names none is the same for every part. Nothing has to cross between parts.
Inputs may be any that keep to these rules, and one draw needn't show every extreme that they name: `segment`: in each micro-batch the ids never fall, each of the 4 pairs holds 24 to 96 consecutive tokens, and one pair holds exactly 96.
All inputs are finite; a program needn't handle non-finite values.
Results may differ from the reference program's by a relative error of at most 0.013.
Values may be sent and summed in bfloat16 or wider, within the bound.
A program may use at most 128 MiB of HBM per device.

```python
import jax
import jax.numpy as jnp
from jax import lax

D = 1024
HEADS = 16
KV_HEADS = 8
HD = 128
TOK_DEV = 192
TICKS = 4
SECTIONS = 16
MAX_LEN = 96
MIN_LEN = 24


def one_batch(key):
    first_key, second_key = jax.random.split(key)
    extra = TOK_DEV // 8
    cuts = jax.random.randint(first_key, (2,), 0, extra + 1)
    lower_cut = jnp.minimum(cuts[0], cuts[1])
    upper_cut = jnp.maximum(cuts[0], cuts[1])
    smaller = jnp.stack([lower_cut, upper_cut - lower_cut, extra - upper_cut]) + MIN_LEN
    longest_at = jax.random.randint(second_key, (), 0, 4)
    lengths = []
    for slot in range(4):
        before = smaller[min(slot, 2)]
        after = smaller[max(slot - 1, 0)]
        pick = jnp.where(slot < longest_at, before, jnp.where(slot == longest_at, MAX_LEN, after))
        lengths.append(pick.astype(jnp.int32))
    ends = jnp.cumsum(jnp.stack(lengths)).astype(jnp.int32)
    where_at = jnp.arange(TOK_DEV, dtype=jnp.int32)
    return jnp.sum((where_at[:, None] >= ends[None, :3]).astype(jnp.int32), axis=1).astype(jnp.int32)


def draw_segment(key, part):
    keys = jax.random.split(key, SECTIONS)
    return jax.vmap(one_batch)(keys)


def steps_of(stream_key, dims, shards, least, high):
    loudness = 1.0
    for dim, shards_of in shards:
        steps = jax.random.uniform(jax.random.fold_in(jax.random.fold_in(stream_key, 6), dim), (shards_of,), jnp.float32, least / len(shards), high / len(shards))
        loudness = loudness * jnp.repeat(jnp.exp(steps), dims[dim] // shards_of).reshape((-1,) + (1,) * (len(dims) - 1 - dim))
    return loudness


def normal_values(key, extent, width, reach, pieces=(), held_as=jnp.bfloat16):
    factor_of = steps_of(key, extent, pieces, -0.22, 0.18) if pieces else 1.0
    values = jax.random.normal(key, extent, jnp.float32) * width * factor_of
    return jnp.minimum(jnp.maximum(values, -reach), reach).astype(held_as)


def setup_inputs(seed: int = 0, part: int = 0) -> dict:
    key_list = jax.random.split(jax.random.key(seed), 8)
    part_splits = jax.random.split(jax.random.fold_in(key_list[7], part), 8)
    micro = normal_values(part_splits[0], (SECTIONS, TOK_DEV, D), 1.0, 6.0, ((0, 16),))
    segment = draw_segment(jax.random.fold_in(jax.random.fold_in(key_list[7], part), 71), part)
    gain = jnp.clip(1.0 + 0.18 * jax.random.normal(key_list[2], (SECTIONS, D), jnp.float32), 0.099609375, 1.8984375).astype(jnp.bfloat16)
    w_query = normal_values(key_list[3], (SECTIONS, D, HEADS * HD), D ** -0.5, 0.1875, ((0, 16),))
    w_key = normal_values(key_list[4], (SECTIONS, D, KV_HEADS * HD), D ** -0.5, 0.1875, ((0, 16),))
    w_value = normal_values(key_list[5], (SECTIONS, D, KV_HEADS * HD), D ** -0.5, 0.1875, ((0, 16),))
    w_out = normal_values(key_list[6], (SECTIONS, HEADS * HD, D), (HEADS * HD) ** -0.5, 0.125, ((0, 16),))
    return {"micro": micro, "segment": segment, "gain": gain, "w_query": w_query, "w_key": w_key, "w_value": w_value, "w_out": w_out}


def positions(pair_ids):
    length = pair_ids.shape[0]
    matched = pair_ids[:, None] == pair_ids[None, :]
    row_index = lax.broadcasted_iota(jnp.int32, (length, length), 0)
    column = lax.broadcasted_iota(jnp.int32, (length, length), 1)
    earlier = matched & (column < row_index)
    places = lax.optimization_barrier(jnp.sum(earlier.astype(jnp.float32), axis=1))
    allowed = matched & (column <= row_index)
    return (places, allowed)

def rotate(values, places):
    middle = values.shape[2] // 2
    ladder = jnp.arange(middle, dtype=jnp.float32)
    spacing = 1000000.0 ** (-2.0 * ladder / (2 * middle))
    angles = places[:, None, None] * spacing[None, None, :]
    cosine = jnp.cos(angles)
    sine_part = jnp.sin(angles)
    front_part = values[:, :, :middle]
    second = values[:, :, middle:]
    return jnp.concatenate([front_part * cosine - second * sine_part, second * cosine + front_part * sine_part], axis=2)

def apply_layer(stream, pair_ids, gain_row, wq_layer, wk_layer, wv_layer, wo_layer):
    length = stream.shape[0]
    stream_f = stream.astype(jnp.float32)
    scale = lax.rsqrt(lax.optimization_barrier(jnp.mean(stream_f * stream_f, axis=1, keepdims=True)) + 1e-05)
    normed = (stream_f * scale * gain_row.astype(jnp.float32)[None, :]).astype(jnp.bfloat16)
    places, allowed = positions(pair_ids)
    queries = rotate(jnp.dot(normed, wq_layer, preferred_element_type=jnp.float32).reshape(length, HEADS, HD), places).astype(jnp.bfloat16)
    key_rows = rotate(jnp.dot(normed, wk_layer, preferred_element_type=jnp.float32).reshape(length, KV_HEADS, HD), places).astype(jnp.bfloat16)
    value_rows = jnp.dot(normed, wv_layer, preferred_element_type=jnp.float32).reshape(length, KV_HEADS, HD).astype(jnp.bfloat16)
    grouped = queries.reshape(length, KV_HEADS, HEADS // KV_HEADS, HD)
    scores = jnp.einsum('ikgd,jkd->kgij', grouped.astype(jnp.float32), key_rows.astype(jnp.float32)) * HD ** (-0.5)
    expo = jnp.where(allowed[None, None], jnp.exp(scores), jnp.zeros_like(scores))
    totals = lax.optimization_barrier(jnp.sum(expo, axis=3, keepdims=True))
    shares = (expo / totals).astype(jnp.bfloat16)
    mixed = jnp.einsum('kgij,jkd->ikgd', shares.astype(jnp.float32), value_rows.astype(jnp.float32)).astype(jnp.bfloat16)
    mixed = mixed.reshape(length, HEADS * HD)
    return (stream_f + jnp.dot(mixed, wo_layer, preferred_element_type=jnp.float32)).astype(jnp.bfloat16)

def reference(micro, segment, gain, w_query, w_key, w_value, w_out):

    def one_section(section_now):
        anchor = (section_now - (TICKS - 1)) % SECTIONS
        stream = micro[anchor]
        pair_ids = segment[anchor]
        for tick_index in range(TICKS):
            layer_at = (anchor + tick_index) % SECTIONS
            stream = apply_layer(stream, pair_ids, gain[layer_at], w_query[layer_at], w_key[layer_at], w_value[layer_at], w_out[layer_at])
        return stream
    return lax.map(one_section, jnp.arange(SECTIONS, dtype=jnp.int32))
```

```python
import functools
import math

import jax
import jax.numpy as jnp
import numpy as np
from jax import lax
from jax.experimental import pallas as pl
from jax.experimental.pallas import tpu as pltpu
from jax.sharding import PartitionSpec as P

HEADS = 16
KV_HEADS = 8
HD = 128
TICKS = 4
CUT = 96
BAND = 96
MESH = pl.DeviceIdType.MESH
GROUP = 4 * HD


def rope_table(length):
    spacing = 1000000.0 ** (-2.0 * np.arange(HD // 2) / HD)
    angles = np.arange(length)[:, None] * spacing[None, :]
    cosine, sine = np.cos(angles), np.sin(angles)
    full = np.concatenate([cosine, cosine, -sine, sine], axis=1).astype(np.float32)
    high = full.astype(jnp.bfloat16)
    low = (full - high.astype(np.float32)).astype(jnp.bfloat16)
    return np.concatenate([high, low], axis=1)


def blocks_of(start, stop):
    if start == 0:
        return [(0, stop, 0, stop)]
    rows = 128 - BAND
    return [(r, r + rows, r - BAND, r + rows) for r in range(start, stop, rows)]


def kernel(
    length, chunks,
    micro, ids, gain_hbm, table_hbm, wq, wk, wv, wo, out,
    xbuf, ybuf, idbuf, gain, table, wqkv, wout,
    normed, qs, ks, vs, mixed, cosine, sine, bias,
    wsem, osem, lsem, send, recv, id_send, id_recv,
):
    n = lax.axis_size("section")
    me = lax.axis_index("section")
    right, left = lax.rem(me + 1, n), lax.rem(me + n - 1, n)

    def local(src, dst, sem):
        return pltpu.make_async_copy(src, dst, sem)

    small = [
        local(ids, idbuf.at[0], lsem.at[0]),
        local(table_hbm, table, lsem.at[1]),
        local(micro.at[0], xbuf.at[0], lsem.at[2]),
        local(gain_hbm, gain, lsem.at[3]),
    ]
    for copy in small:
        copy.start()

    def group_copies(g):
        q_at = pl.ds(g * 2 * HD, 2 * HD)
        k_at = pl.ds(g * HD, HD)
        return (
            local(wq.at[0, :, q_at], wqkv.at[g, :, 0 : 2 * HD], wsem.at[g, 0]),
            local(wk.at[0, :, k_at], wqkv.at[g, :, 2 * HD : 3 * HD], wsem.at[g, 1]),
            local(wv.at[0, :, k_at], wqkv.at[g, :, 3 * HD :], wsem.at[g, 2]),
        )

    for g in range(KV_HEADS):
        for copy in group_copies(g):
            copy.start()
    out_copy = local(wo.at[0], wout, osem)
    out_copy.start()

    barrier = pltpu.get_barrier_semaphore()
    pl.semaphore_signal(barrier, inc=1, device_id={"section": left}, device_id_type=MESH)
    pl.semaphore_wait(barrier, 1)
    for copy in small:
        copy.wait()

    def rows_copy(t, c):
        at = pl.ds(chunks[c][0], chunks[c][1] - chunks[c][0])
        return pltpu.make_async_remote_copy(
            ybuf.at[t, at, :], xbuf.at[t + 1, at, :], send.at[t, c], recv.at[t, c],
            device_id={"section": right}, device_id_type=MESH,
        )

    def id_copy(t):
        return pltpu.make_async_remote_copy(
            idbuf.at[t], idbuf.at[t + 1], id_send.at[t], id_recv.at[t],
            device_id={"section": right}, device_id_type=MESH,
        )

    def places(t):
        row = idbuf[t].astype(jnp.float32)
        i = lax.broadcasted_iota(jnp.int32, (length, length), 0)
        j = lax.broadcasted_iota(jnp.int32, (length, length), 1)
        across = jnp.broadcast_to(row, (length, length))
        down = jnp.sum(jnp.where(i == j, across, 0.0), axis=1, keepdims=True)
        matched = across == down
        place = jnp.sum(jnp.where(matched & (j < i), 1.0, 0.0), axis=1, keepdims=True)
        chosen = jnp.where(j.astype(jnp.float32) == place, 1.0, 0.0).astype(jnp.bfloat16)
        turns = jnp.dot(chosen, table[...], preferred_element_type=jnp.float32)
        cosine[...] = turns[:, :HD] + turns[:, 2 * HD : 3 * HD]
        sine[...] = turns[:, HD : 2 * HD] + turns[:, 3 * HD :]
        limits = jnp.where(matched & (j <= i), 0.0, -1e30)
        for start, stop in chunks:
            for r0, r1, k0, k1 in blocks_of(start, stop):
                bias[r0:r1, 0 : k1 - k0] = limits[r0:r1, k0:k1]

    def turn(x, rows):
        return (x * cosine[rows, :] + pltpu.roll(x, HD // 2, 1) * sine[rows, :]).astype(jnp.bfloat16)

    def project(g, start, stop):
        rows = pl.ds(start, stop - start)
        return jnp.dot(normed[rows, :], wqkv[g], preferred_element_type=jnp.float32)

    def keep(g, start, stop, made):
        rows = pl.ds(start, stop - start)
        qs[g, 0, rows, :] = turn(made[:, :HD], rows)
        qs[g, 1, rows, :] = turn(made[:, HD : 2 * HD], rows)
        ks[g, rows, :] = turn(made[:, 2 * HD : 3 * HD], rows)
        vs[g, rows, :] = made[:, 3 * HD :].astype(jnp.bfloat16)

    def attend(g, start, stop):
        for r0, r1, k0, k1 in blocks_of(start, stop):
            count, width = r1 - r0, k1 - k0
            q = qs[g, :, r0:r1, :].reshape(2 * count, HD)
            scores = lax.dot_general(
                q, ks[g, k0:k1, :], (((1,), (1,)), ((), ())), preferred_element_type=jnp.float32
            ).reshape(2, count, width)
            expo = jnp.exp2(scores * (HD ** -0.5 * math.log2(math.e)) + bias[r0:r1, 0:width][None])
            shares = (expo / jnp.sum(expo, axis=2, keepdims=True)).astype(jnp.bfloat16)
            got = jnp.dot(
                shares.reshape(2 * count, width), vs[g, k0:k1, :], preferred_element_type=jnp.float32
            ).astype(jnp.bfloat16)
            both = jnp.concatenate([got[:count], got[count:]], axis=1)
            mixed[r0:r1, pl.ds(pl.multiple_of(g * 2 * HD, 2 * HD), 2 * HD)] = both

    def tick(t, first, waits):
        if not first:
            id_copy(t - 1).wait_recv()

        def forward():
            id_copy(t).start()

        if first:
            forward()
        else:
            pl.when(t < TICKS - 1)(forward)
        places(t)
        for c, (start, stop) in enumerate(chunks):
            rows = pl.ds(start, stop - start)
            if not first:
                rows_copy(t - 1, c).wait_recv()
            x = xbuf[t, rows, :].astype(jnp.float32)
            scale = lax.rsqrt(jnp.mean(x * x, axis=1, keepdims=True) + 1e-05)
            normed[rows, :] = (x * scale * gain[...].astype(jnp.float32)).astype(jnp.bfloat16)
            load = first and c == 0

            def ready(g):
                if load:
                    for copy in group_copies(g):
                        copy.wait()

            ready(0)
            keep(0, start, stop, project(0, start, stop))

            def step(g, carry):
                ready(g + 1)
                made = project(g + 1, start, stop)
                attend(g, start, stop)
                keep(g + 1, start, stop, made)
                return carry

            if load:
                for g in range(KV_HEADS - 1):
                    step(g, 0)
            else:
                lax.fori_loop(0, KV_HEADS - 1, step, 0)
            attend(KV_HEADS - 1, start, stop)
            if load:
                out_copy.wait()
            width = 256
            for at in range(0, ybuf.shape[2], width):
                update = jnp.dot(
                    mixed[rows, :], wout[:, at : at + width], preferred_element_type=jnp.float32
                )
                ybuf[t, rows, at : at + width] = (
                    xbuf[t, rows, at : at + width].astype(jnp.float32) + update
                ).astype(jnp.bfloat16)
            if first:
                rows_copy(t, c).start()
            else:
                pl.when(t < TICKS - 1)(rows_copy(t, c).start)

    tick(0, True, True)

    def later(t, carry):
        tick(t, False, False)
        return carry

    lax.fori_loop(1, TICKS, later, 0)
    out[0] = ybuf[TICKS - 1]
    for t in range(TICKS - 1):
        id_copy(t).wait_send()
        for c in range(len(chunks)):
            rows_copy(t, c).wait_send()


def body(micro, segment, gain, w_query, w_key, w_value, w_out):
    _, length, width = micro.shape
    chunks = [(0, CUT), (CUT, length)]
    table = jnp.asarray(rope_table(length))
    bf, f32 = jnp.bfloat16, jnp.float32
    count = len(chunks)
    any_space = pl.BlockSpec(memory_space=pl.ANY)
    vmem = pl.BlockSpec(memory_space=pltpu.VMEM)
    return pl.pallas_call(
        functools.partial(kernel, length, chunks),
        out_shape=jax.ShapeDtypeStruct((1, length, width), bf),
        in_specs=[any_space] * 8,
        out_specs=vmem,
        scratch_shapes=[
            pltpu.VMEM((TICKS, length, width), bf),
            pltpu.VMEM((TICKS, length, width), bf),
            pltpu.VMEM((TICKS, 1, length), jnp.int32),
            pltpu.VMEM((1, width), bf),
            pltpu.VMEM(table.shape, bf),
            pltpu.VMEM((KV_HEADS, width, GROUP), bf),
            pltpu.VMEM((HEADS * HD, width), bf),
            pltpu.VMEM((length, width), bf),
            pltpu.VMEM((KV_HEADS, 2, length, HD), bf),
            pltpu.VMEM((KV_HEADS, length, HD), bf),
            pltpu.VMEM((KV_HEADS, length, HD), bf),
            pltpu.VMEM((length, HEADS * HD), bf),
            pltpu.VMEM((length, HD), f32),
            pltpu.VMEM((length, HD), f32),
            pltpu.VMEM((length, HD), f32),
            pltpu.SemaphoreType.DMA((KV_HEADS, 3)),
            pltpu.SemaphoreType.DMA,
            pltpu.SemaphoreType.DMA((4,)),
            pltpu.SemaphoreType.DMA((TICKS - 1, count)),
            pltpu.SemaphoreType.DMA((TICKS - 1, count)),
            pltpu.SemaphoreType.DMA((TICKS - 1,)),
            pltpu.SemaphoreType.DMA((TICKS - 1,)),
        ],
        compiler_params=pltpu.CompilerParams(
            collective_id=0, has_side_effects=True, vmem_limit_bytes=60 * 1024 * 1024
        ),
    )(micro, segment, gain, table, w_query, w_key, w_value, w_out)


def solution(mesh):
    in_specs = (
        P(("groups", "section"), None, None),
        P(("groups", "section"), None),
        P("section", None),
        P("section", None, None),
        P("section", None, None),
        P("section", None, None),
        P("section", None, None),
    )
    out_specs = P(("groups", "section"), None, None)
    return jax.shard_map(body, mesh=mesh, in_specs=in_specs, out_specs=out_specs, check_vma=False)
```

```python
import functools
import math

import jax
import jax.numpy as jnp
import numpy as np
from jax import lax
from jax.experimental import pallas as pl
from jax.experimental.pallas import tpu as pltpu
from jax.sharding import PartitionSpec as P

HEADS = 16
KV_HEADS = 8
HD = 128
TICKS = 4
PIECES = 4
BAND = 96
MESH = pl.DeviceIdType.MESH
GROUP = 4 * HD


def rope_table(length):
    spacing = 1000000.0 ** (-2.0 * np.arange(HD // 2) / HD)
    angles = np.arange(length)[:, None] * spacing[None, :]
    cosine, sine = np.cos(angles), np.sin(angles)
    full = np.concatenate([cosine, cosine, -sine, sine], axis=1).astype(np.float32)
    high = full.astype(jnp.bfloat16)
    low = (full - high.astype(np.float32)).astype(jnp.bfloat16)
    return np.concatenate([high, low], axis=1)


def blocks_of(start, stop):
    rows = 128 - BAND
    later = [(r, r + rows, r - BAND, r + rows) for r in range(128, stop, rows)]
    return [(0, 128, 0, 128)] + later


def kernel(
    length, chunks,
    micro, ids, gain_hbm, table_hbm, wq, wk, wv, wo, out,
    xbuf, ybuf, idbuf, gain, table, wqkv, wout,
    normed, qs, ks, vs, mixed, cosine, sine, bias,
    wsem, osem, lsem, send, recv, id_send, id_recv,
):
    n = lax.axis_size("section")
    me = lax.axis_index("section")
    right, left = lax.rem(me + 1, n), lax.rem(me + n - 1, n)

    def local(src, dst, sem):
        return pltpu.make_async_copy(src, dst, sem)

    small = [
        local(ids, idbuf.at[0], lsem.at[0]),
        local(table_hbm, table, lsem.at[1]),
        local(micro.at[0], xbuf.at[0], lsem.at[2]),
        local(gain_hbm, gain, lsem.at[3]),
    ]
    for copy in small:
        copy.start()

    def group_copies(g):
        q_at = pl.ds(g * 2 * HD, 2 * HD)
        k_at = pl.ds(g * HD, HD)
        return (
            local(wq.at[0, :, q_at], wqkv.at[g, :, 0 : 2 * HD], wsem.at[g, 0]),
            local(wk.at[0, :, k_at], wqkv.at[g, :, 2 * HD : 3 * HD], wsem.at[g, 1]),
            local(wv.at[0, :, k_at], wqkv.at[g, :, 3 * HD :], wsem.at[g, 2]),
        )

    for g in range(KV_HEADS):
        for copy in group_copies(g):
            copy.start()
    out_copy = local(wo.at[0], wout, osem)
    out_copy.start()

    barrier = pltpu.get_barrier_semaphore()
    pl.semaphore_signal(barrier, inc=1, device_id={"section": left}, device_id_type=MESH)
    pl.semaphore_wait(barrier, 1)
    for copy in small:
        copy.wait()

    def piece_copy(t, c):
        width = ybuf.shape[2] // PIECES
        at = pl.ds(c * width, width)
        return pltpu.make_async_remote_copy(
            ybuf.at[t, :, at], xbuf.at[t + 1, :, at], send.at[t, c], recv.at[t, c],
            device_id={"section": right}, device_id_type=MESH,
        )

    def id_copy(t):
        return pltpu.make_async_remote_copy(
            idbuf.at[t], idbuf.at[t + 1], id_send.at[t], id_recv.at[t],
            device_id={"section": right}, device_id_type=MESH,
        )

    def places(t):
        row = idbuf[t].astype(jnp.float32)
        i = lax.broadcasted_iota(jnp.int32, (length, length), 0)
        j = lax.broadcasted_iota(jnp.int32, (length, length), 1)
        across = jnp.broadcast_to(row, (length, length))
        down = jnp.sum(jnp.where(i == j, across, 0.0), axis=1, keepdims=True)
        matched = across == down
        place = jnp.sum(jnp.where(matched & (j < i), 1.0, 0.0), axis=1, keepdims=True)
        chosen = jnp.where(j.astype(jnp.float32) == place, 1.0, 0.0).astype(jnp.bfloat16)
        turns = jnp.dot(chosen, table[...], preferred_element_type=jnp.float32)
        cosine[...] = turns[:, :HD] + turns[:, 2 * HD : 3 * HD]
        sine[...] = turns[:, HD : 2 * HD] + turns[:, 3 * HD :]
        limits = jnp.where(matched & (j <= i), 0.0, -1e30)
        for start, stop in chunks:
            for r0, r1, k0, k1 in blocks_of(start, stop):
                bias[r0:r1, 0 : k1 - k0] = limits[r0:r1, k0:k1]

    def turn(x, rows):
        return (x * cosine[rows, :] + pltpu.roll(x, HD // 2, 1) * sine[rows, :]).astype(jnp.bfloat16)

    def project(g, start, stop):
        rows = pl.ds(start, stop - start)
        return jnp.dot(normed[rows, :], wqkv[g], preferred_element_type=jnp.float32)

    def keep(g, start, stop, made):
        rows = pl.ds(start, stop - start)
        qs[g, 0, rows, :] = turn(made[:, :HD], rows)
        qs[g, 1, rows, :] = turn(made[:, HD : 2 * HD], rows)
        ks[g, rows, :] = turn(made[:, 2 * HD : 3 * HD], rows)
        vs[g, rows, :] = made[:, 3 * HD :].astype(jnp.bfloat16)

    def attend(g, start, stop):
        for r0, r1, k0, k1 in blocks_of(start, stop):
            count, width = r1 - r0, k1 - k0
            q = qs[g, :, r0:r1, :].reshape(2 * count, HD)
            scores = lax.dot_general(
                q, ks[g, k0:k1, :], (((1,), (1,)), ((), ())), preferred_element_type=jnp.float32
            ).reshape(2, count, width)
            expo = jnp.exp2(scores * (HD ** -0.5 * math.log2(math.e)) + bias[r0:r1, 0:width][None])
            shares = (expo / jnp.sum(expo, axis=2, keepdims=True)).astype(jnp.bfloat16)
            got = jnp.dot(
                shares.reshape(2 * count, width), vs[g, k0:k1, :], preferred_element_type=jnp.float32
            ).astype(jnp.bfloat16)
            both = jnp.concatenate([got[:count], got[count:]], axis=1)
            mixed[r0:r1, pl.ds(pl.multiple_of(g * 2 * HD, 2 * HD), 2 * HD)] = both

    def tick(t, first, waits):
        if not first:
            id_copy(t - 1).wait_recv()

        def forward():
            id_copy(t).start()

        if first:
            forward()
        else:
            pl.when(t < TICKS - 1)(forward)
        places(t)
        for c, (start, stop) in enumerate(chunks):
            rows = pl.ds(start, stop - start)
            if not first:
                for piece in range(PIECES):
                    piece_copy(t - 1, piece).wait_recv()
            x = xbuf[t, rows, :].astype(jnp.float32)
            scale = lax.rsqrt(jnp.mean(x * x, axis=1, keepdims=True) + 1e-05)
            normed[rows, :] = (x * scale * gain[...].astype(jnp.float32)).astype(jnp.bfloat16)
            load = first and c == 0

            def ready(g):
                if load:
                    for copy in group_copies(g):
                        copy.wait()

            ready(0)
            keep(0, start, stop, project(0, start, stop))

            def step(g, carry):
                ready(g + 1)
                made = project(g + 1, start, stop)
                attend(g, start, stop)
                keep(g + 1, start, stop, made)
                return carry

            if load:
                for g in range(KV_HEADS - 1):
                    step(g, 0)
            else:
                lax.fori_loop(0, KV_HEADS - 1, step, 0)
            attend(KV_HEADS - 1, start, stop)
            if load:
                out_copy.wait()
            width = ybuf.shape[2] // PIECES
            for piece in range(PIECES):
                at = piece * width
                update = jnp.dot(
                    mixed[rows, :], wout[:, at : at + width], preferred_element_type=jnp.float32
                )
                ybuf[t, rows, at : at + width] = (
                    xbuf[t, rows, at : at + width].astype(jnp.float32) + update
                ).astype(jnp.bfloat16)
                if first:
                    piece_copy(t, piece).start()
                else:
                    pl.when(t < TICKS - 1)(piece_copy(t, piece).start)

    tick(0, True, True)

    def later(t, carry):
        tick(t, False, False)
        return carry

    lax.fori_loop(1, TICKS, later, 0)
    out[0] = ybuf[TICKS - 1]
    for t in range(TICKS - 1):
        id_copy(t).wait_send()
        for piece in range(PIECES):
            piece_copy(t, piece).wait_send()


def body(micro, segment, gain, w_query, w_key, w_value, w_out):
    _, length, width = micro.shape
    chunks = [(0, length)]
    table = jnp.asarray(rope_table(length))
    bf, f32 = jnp.bfloat16, jnp.float32
    any_space = pl.BlockSpec(memory_space=pl.ANY)
    vmem = pl.BlockSpec(memory_space=pltpu.VMEM)
    return pl.pallas_call(
        functools.partial(kernel, length, chunks),
        out_shape=jax.ShapeDtypeStruct((1, length, width), bf),
        in_specs=[any_space] * 8,
        out_specs=vmem,
        scratch_shapes=[
            pltpu.VMEM((TICKS, length, width), bf),
            pltpu.VMEM((TICKS, length, width), bf),
            pltpu.VMEM((TICKS, 1, length), jnp.int32),
            pltpu.VMEM((1, width), bf),
            pltpu.VMEM(table.shape, bf),
            pltpu.VMEM((KV_HEADS, width, GROUP), bf),
            pltpu.VMEM((HEADS * HD, width), bf),
            pltpu.VMEM((length, width), bf),
            pltpu.VMEM((KV_HEADS, 2, length, HD), bf),
            pltpu.VMEM((KV_HEADS, length, HD), bf),
            pltpu.VMEM((KV_HEADS, length, HD), bf),
            pltpu.VMEM((length, HEADS * HD), bf),
            pltpu.VMEM((length, HD), f32),
            pltpu.VMEM((length, HD), f32),
            pltpu.VMEM((length, HD), f32),
            pltpu.SemaphoreType.DMA((KV_HEADS, 3)),
            pltpu.SemaphoreType.DMA,
            pltpu.SemaphoreType.DMA((4,)),
            pltpu.SemaphoreType.DMA((TICKS - 1, PIECES)),
            pltpu.SemaphoreType.DMA((TICKS - 1, PIECES)),
            pltpu.SemaphoreType.DMA((TICKS - 1,)),
            pltpu.SemaphoreType.DMA((TICKS - 1,)),
        ],
        compiler_params=pltpu.CompilerParams(
            collective_id=0, has_side_effects=True, vmem_limit_bytes=60 * 1024 * 1024
        ),
    )(micro, segment, gain, table, w_query, w_key, w_value, w_out)


def solution(mesh):
    in_specs = (
        P(("groups", "section"), None, None),
        P(("groups", "section"), None),
        P("section", None),
        P("section", None, None),
        P("section", None, None),
        P("section", None, None),
        P("section", None, None),
    )
    out_specs = P(("groups", "section"), None, None)
    return jax.shard_map(body, mesh=mesh, in_specs=in_specs, out_specs=out_specs, check_vma=False)
```
